32 devices in a mesh: leaf: 32 (over z, y, x, core).
Axes of the slice: x: 2, y: 2, z: 4, core: 2. Of those that a mesh axis runs over, the one named last changes fastest.
Arguments:
- vectors: float32 [16, 131072], P(None, 'leaf'), may hold values from -6 to 6
- morton_order: int32 [32, 4096], P('leaf'), may hold values from 0 to 4095, each once within a row
- leaf_sizes: int32 [32, 32], P('leaf'), may hold values from 1 to 256, 4096 in all within a row
- leaf_basis: bfloat16 [32, 131072], P(None, 'leaf'), may hold values from -0.5 to 0.5
- leaf_transfer: bfloat16 [1024, 1024], P('leaf'), may hold values from -0.75 to 0.75
- mid_transfer: bfloat16 [128, 1024], P('leaf'), may hold values from -1 to 1
- root_transfer: bfloat16 [32, 1024], P('leaf'), may hold values from -0.75 to 0.75
- leaf_pairs: int32 [2, 2048], P(None, 'leaf'), may hold values from 0 to 31, as said below
- leaf_coupling: bfloat16 [2048, 1024], P('leaf'), may hold values from -0.5 to 0.5
- dev_partner: int32 [32, 16], P('leaf'), may hold values from -1 to 31, as said below
- dev_coupling: bfloat16 [512, 1024], P('leaf'), may hold values from -0.25 to 0.25
- grp_partner: int32 [32, 4], P('leaf'), may hold values from 0 to 3, as said below
- grp_coupling: bfloat16 [128, 1024], P('leaf'), may hold values from -0.5 to 0.5
Outputs:
- far_field: float32 [16, 131072], P(None, 'leaf')
The draws below stay inside these ranges and needn't reach their ends.
Inputs may be any that keep to these rules, and one draw needn't show every extreme that they name: `morton_order`: each row is a permutation of 0 to 4095. `leaf_pairs`: the two leaves of a pair differ. `dev_partner`: live entries of a row come first, are distinct and never the row's own subtree; an unordered pair of subtrees appears in at most one slot of all rows; some row has all 16 slots live. `grp_partner`: never the device's own group.
All inputs are finite; a program needn't handle non-finite values.
Results may differ from the reference program's by a relative error of at most 0.014.
Values may be sent and summed in bfloat16 or wider, within the bound.
No kernel may reach another device: no remote copies, remote signals or barrier semaphores. Data moves between devices by JAX's collectives and lax.ppermute only.
A program may use at most 64 MiB of HBM per device.

```python
import math
import jax
import jax.numpy as jnp
import numpy as np
from jax import lax

RANK = 32
LEAF = 256
VECS = 16
LEAVES_DEV = 32
LPAIRS = 64
GCAP = 4
PTS_DEV = 4096
MIDS_DEV = 4
SUBTREES = 32
GROUPS = 4
PCAP = 16
POINTS = 131072
LEAVES = 1024
MIDS = 128


def draw_leaf_pairs(key, part):
    base_key = jax.random.fold_in(key, 31)
    first_key, step_key = jax.random.split(base_key)
    first_leaf = jax.random.randint(first_key, (SUBTREES * LPAIRS,), 0, LEAVES_DEV)
    offset = jax.random.randint(step_key, (SUBTREES * LPAIRS,), 1, LEAVES_DEV)
    second = (first_leaf + offset) % LEAVES_DEV
    return jnp.stack([first_leaf, second]).astype(jnp.int32)


def draw_grp_partner(key, part):
    base_key = jax.random.fold_in(key, 47)
    offset = jax.random.randint(base_key, (SUBTREES, GCAP), 1, GROUPS)
    own_group = (jnp.arange(SUBTREES, dtype=jnp.int32) // 8)[:, None]
    return ((own_group + offset) % GROUPS).astype(jnp.int32)


def draw_dev_partner(key, part):
    base_key = jax.random.fold_in(key, 59)
    perm_key, score_key, count_key = jax.random.split(base_key, 3)
    ranking = jax.random.permutation(perm_key, SUBTREES).astype(jnp.int32)
    scores = jax.random.randint(score_key, (SUBTREES, SUBTREES), 0, 1 << 20) * SUBTREES + jnp.arange(SUBTREES, dtype=jnp.int32)[None, :]
    allowed = ranking[None, :] > ranking[:, None]
    scores = jnp.where(allowed, scores, -1)
    top_score, top_index = lax.top_k(scores, PCAP)
    counts = jax.random.randint(count_key, (SUBTREES,), 1, PCAP + 1)
    counts = jnp.where(ranking == 0, PCAP, counts)
    slots = jnp.arange(PCAP, dtype=jnp.int32)[None, :]
    is_live = (top_score >= 0) & (slots < counts[:, None])
    return jnp.where(is_live, top_index, -1).astype(jnp.int32)


def level_of(stream_key, shape, cuts, low, top_value):
    factor_of, own = 1.0, jax.random.fold_in(stream_key, 6)
    for position, blocks in cuts:
        heights = jnp.exp(jax.random.uniform(jax.random.fold_in(own, position), (blocks,), jnp.float32, low / len(cuts), top_value / len(cuts)))
        factor_of = factor_of * jnp.repeat(heights, shape[position] // blocks).reshape([-1 if axis == position else 1 for axis in range(len(shape))])
    return factor_of


def length_profile(amount, total, reach, slope):
    weights = [(1 << 20) // math.isqrt(rank ** slope) + 1 for rank in range(2, amount + 1)]
    spare, given = total - reach - (amount - 1), [1] * (amount - 1)
    while spare > 0:
        candidates = [i for i in range(amount - 1) if given[i] < reach]
        mass, budget = sum([weights[i] for i in candidates]), spare
        for i in candidates:
            more = min(reach - given[i], max(1, budget * weights[i] // mass), spare)
            given[i] = given[i] + more
            spare = spare - more
    return np.array([reach] + given)


def uneven_parts(stream_key, amount, total, limit, skew):
    if amount == 2:
        one = jax.random.randint(stream_key, (), max(1, total - limit), min(limit, total - 1) + 1)
        return jnp.stack([one, total - one])
    lengths = jnp.asarray(length_profile(amount, total, limit, skew), jnp.int32)
    twos = (amount - 1) // 2
    donor, taker = lengths[1:1 + 2 * twos:2], lengths[2:2 + 2 * twos:2]
    room = jnp.minimum(donor - 1, limit - taker)
    shifted = jax.random.randint(jax.random.fold_in(stream_key, 1), (twos,), 0, 1 << 20) % (room + 1)
    lengths = lengths.at[1:1 + 2 * twos:2].set(donor - shifted).at[2:2 + 2 * twos:2].set(taker + shifted)
    return lengths[jax.random.permutation(jax.random.fold_in(stream_key, 2), amount)]


def scatter_about(rng, dims, deviation, bound, pieces=(), kind=jnp.bfloat16):
    values = deviation * jax.random.normal(rng, dims, jnp.float32)
    if pieces:
        values = values * level_of(rng, dims, pieces, -0.22, 0.18)
    return jnp.clip(values, -bound, bound).astype(kind)


def setup_inputs(seed: int = 0) -> dict:
    seeds = jax.random.split(jax.random.key(seed), 14)
    vectors = scatter_about(seeds[0], (VECS, POINTS), 1.0, 6.0, ((1, 32),), jnp.float32)
    morton_order = jax.vmap(lambda own: jax.random.permutation(own, PTS_DEV))(jax.random.split(seeds[1], SUBTREES)).reshape((SUBTREES, PTS_DEV)).astype(jnp.int32)
    leaf_sizes = jax.vmap(lambda own: uneven_parts(own, LEAVES_DEV, PTS_DEV, LEAF, 1))(jax.random.split(seeds[2], SUBTREES)).reshape((SUBTREES, LEAVES_DEV)).astype(jnp.int32)
    leaf_basis = scatter_about(seeds[3], (RANK, POINTS), (LEAF // 2) ** -0.5, 0.5, ((1, 32),))
    leaf_transfer = scatter_about(seeds[4], (LEAVES, RANK * RANK), (2 * RANK) ** -0.5, 0.75, ((0, 32),))
    mid_transfer = scatter_about(seeds[5], (MIDS, RANK * RANK), (RANK * MIDS_DEV // 4) ** -0.5, 1.0, ((0, 32),))
    root_transfer = scatter_about(seeds[6], (SUBTREES, RANK * RANK), (2 * RANK) ** -0.5, 0.75, ((0, 32),))
    leaf_pairs = draw_leaf_pairs(jax.random.fold_in(seeds[13], 71), 0)
    leaf_coupling = scatter_about(seeds[8], (SUBTREES * LPAIRS, RANK * RANK), (4 * RANK) ** -0.5, 0.5, ((0, 32),))
    dev_partner = draw_dev_partner(jax.random.fold_in(seeds[13], 71), 0)
    dev_coupling = scatter_about(seeds[10], (SUBTREES * PCAP, RANK * RANK), (16 * RANK) ** -0.5, 0.25, ((0, 32),))
    grp_partner = draw_grp_partner(jax.random.fold_in(seeds[13], 71), 0)
    grp_coupling = scatter_about(seeds[12], (SUBTREES * GCAP, RANK * RANK), (4 * RANK) ** -0.5, 0.5, ((0, 32),))
    return {"vectors": vectors, "morton_order": morton_order, "leaf_sizes": leaf_sizes, "leaf_basis": leaf_basis, "leaf_transfer": leaf_transfer, "mid_transfer": mid_transfer, "root_transfer": root_transfer, "leaf_pairs": leaf_pairs, "leaf_coupling": leaf_coupling, "dev_partner": dev_partner, "dev_coupling": dev_coupling, "grp_partner": grp_partner, "grp_coupling": grp_coupling}


def rounded(value):
    return lax.optimization_barrier(value.astype(jnp.bfloat16)).astype(jnp.float32)


def windows(sizes, total):
    starts = jnp.cumsum(sizes) - sizes
    offset = jnp.arange(LEAF, dtype=jnp.int32)
    places = starts[:, None] + offset[None, :]
    inside = offset[None, :] < sizes[:, None]
    return jnp.minimum(places, total - 1).astype(jnp.int32), inside


def reference(vectors, morton_order, leaf_sizes, leaf_basis, leaf_transfer, mid_transfer, root_transfer, leaf_pairs, leaf_coupling, dev_partner, dev_coupling, grp_partner, grp_coupling):
    subtrees = morton_order.shape[0]
    points = morton_order.shape[1]
    count_vec = vectors.shape[0]
    basis_rank = leaf_basis.shape[0]
    leaves = leaf_sizes.shape[1]
    middle = leaves // 8
    groups = subtrees // 8
    vec_dev = vectors.reshape(count_vec, subtrees, points).transpose(1, 0, 2)
    basis_dev = leaf_basis.reshape(basis_rank, subtrees, points).transpose(1, 0, 2)
    leaf_maps = leaf_transfer.reshape(subtrees, leaves, basis_rank, basis_rank)
    mid_maps = mid_transfer.reshape(subtrees, middle, basis_rank, basis_rank)
    root_maps = root_transfer.reshape(subtrees, basis_rank, basis_rank).astype(jnp.float32)
    pairs_dev = leaf_pairs.reshape(2, subtrees, -1).transpose(1, 0, 2)
    leaf_blocks = leaf_coupling.reshape(subtrees, -1, basis_rank, basis_rank)

    def upward(device_item):
        vec, morton, sizes, basis, lmap, mmap, rmap, pairs, blocks = device_item
        places, inside = windows(sizes, points)
        sorted_vec = vec[:, morton].astype(jnp.bfloat16).astype(jnp.float32)
        basis_win = basis[:, places].astype(jnp.float32)
        vec_win = jnp.where(inside[None], sorted_vec[:, places], 0.0)
        leaf_coeff = rounded(jnp.einsum("rls,vls->lrv", basis_win, vec_win))
        child = jnp.einsum("lij,liv->ljv", lmap.astype(jnp.float32), leaf_coeff)
        mid_coeff = rounded(child.reshape(middle, 8, basis_rank, count_vec).sum(1))
        root_coeff = rounded(jnp.einsum("mij,miv->jv", mmap.astype(jnp.float32), mid_coeff))
        group_term = rounded(jnp.einsum("ij,iv->jv", rmap, root_coeff))
        blockf = blocks.astype(jnp.float32)
        forward = jnp.einsum("pij,pjv->piv", blockf, leaf_coeff[pairs[1]])
        backward = jnp.einsum("pij,piv->pjv", blockf, leaf_coeff[pairs[0]])
        leaf_far = jnp.zeros((leaves, basis_rank, count_vec), jnp.float32)
        leaf_far = leaf_far.at[pairs[0]].add(forward).at[pairs[1]].add(backward)
        return root_coeff, group_term, leaf_far

    root_coeff, group_term, leaf_far = lax.map(upward, (vec_dev, morton_order, leaf_sizes, basis_dev, leaf_maps, mid_maps, root_maps, pairs_dev, leaf_blocks))
    group_coeff = rounded(group_term.reshape(groups, 8, basis_rank, count_vec).sum(1))
    is_live = dev_partner >= 0
    safe_id = jnp.where(is_live, dev_partner, 0).astype(jnp.int32)
    dev_blocks = dev_coupling.reshape(subtrees, -1, basis_rank, basis_rank).astype(jnp.float32)
    chosen = root_coeff[safe_id] * is_live[..., None, None].astype(jnp.float32)
    root_far = jnp.einsum("acij,acjv->aiv", dev_blocks, chosen)
    back = jnp.einsum("acij,aiv->acjv", dev_blocks, root_coeff) * is_live[..., None, None].astype(jnp.float32)
    root_far = root_far.at[safe_id.reshape(-1)].add(back.reshape(-1, basis_rank, count_vec))
    own_group = (jnp.arange(subtrees, dtype=jnp.int32) // 8).astype(jnp.int32)
    grp_blocks = grp_coupling.reshape(subtrees, -1, basis_rank, basis_rank).astype(jnp.float32)
    to_own = jnp.einsum("acij,acjv->aiv", grp_blocks, group_coeff[grp_partner])
    to_far = jnp.einsum("acij,aiv->acjv", grp_blocks, group_coeff[own_group])
    group_far = jnp.zeros((groups, basis_rank, count_vec), jnp.float32)
    group_far = rounded(group_far.at[own_group].add(to_own).at[grp_partner.reshape(-1)].add(to_far.reshape(-1, basis_rank, count_vec)))
    root_total = rounded(root_far + jnp.einsum("aij,ajv->aiv", root_maps, group_far[own_group]))

    def downward(device_item):
        morton, sizes, basis, lmap, mmap, top, near = device_item
        places, inside = windows(sizes, points)
        mid_total = rounded(jnp.einsum("mij,jv->miv", mmap.astype(jnp.float32), top))
        parent = jnp.repeat(mid_total, 8, axis=0)
        leaf_total = rounded(near + jnp.einsum("lij,ljv->liv", lmap.astype(jnp.float32), parent))
        basis_win = basis[:, places].astype(jnp.float32)
        out_win = jnp.where(inside[None], jnp.einsum("rls,lrv->vls", basis_win, leaf_total), 0.0)
        sorted_out = jnp.zeros((count_vec, points), jnp.float32).at[:, places].add(out_win)
        return jnp.zeros((count_vec, points), jnp.float32).at[:, morton].set(sorted_out)

    result = lax.map(downward, (morton_order, leaf_sizes, basis_dev, leaf_maps, mid_maps, root_total, leaf_far))
    return result.transpose(1, 0, 2).reshape(count_vec, subtrees * points)
```

```python
import functools

import jax
import jax.numpy as jnp
from jax import lax
from jax.experimental import pallas as pl
from jax.experimental.pallas import tpu as pltpu
from jax.sharding import PartitionSpec as P

LEAF = 256
SPLIT = 256

bf16 = jnp.bfloat16
f32 = jnp.float32
highest = lax.Precision.HIGHEST


def dot(a, b, over):
    return lax.dot_general(a, b, (over, ((), ())), preferred_element_type=f32)


NN = ((1,), (0,))
NT = ((1,), (1,))
TN = ((0,), (0,))


def one_hot_low(morton, width):
    rows = lax.broadcasted_iota(jnp.int32, (SPLIT, width), 0)
    return jnp.where(rows == (morton & (SPLIT - 1)), 1.0, 0.0).astype(bf16)


def window(start, points, width):
    base = jnp.minimum(start // 128 * 128, points - width)
    return pl.multiple_of(base, 128)


def spread(ref, rank):
    flat = ref[...]
    return jnp.concatenate([flat[:, rank * i : rank * (i + 1)] for i in range(rank)], axis=0)


def spread_into(scr, ref, row, pitch, rank):
    flat = ref[...].astype(f32)
    n = flat.shape[0]
    for i in range(rank):
        scr[i * pitch + row : i * pitch + row + n, :rank] = flat[:, rank * i : rank * (i + 1)]


def up_leaf_kernel(sizes, vec_ref, morton_ref, basis_ref, coeff_ref, sorted_ref, scr):
    vecs, points = vec_ref.shape
    rank = basis_ref.shape[0]
    leaves = sizes.shape[1]
    highs = points // SPLIT
    width = min(points, LEAF + 128)
    stacked = jnp.concatenate(
        [vec_ref[:, h * SPLIT : (h + 1) * SPLIT].astype(bf16) for h in range(highs)], axis=0
    )
    step = 256
    for k in range(points // step):
        morton = morton_ref[:, k * step : (k + 1) * step]
        mixed = dot(stacked, one_hot_low(morton, step), NN)
        high = morton // SPLIT
        picked = jnp.zeros((vecs, step), f32)
        for h in range(highs):
            picked = picked + jnp.where(high == h, mixed[h * vecs : (h + 1) * vecs], 0.0)
        sorted_ref[:, k * step : (k + 1) * step] = picked
    start = jnp.int32(0)
    for l in range(leaves):
        size = sizes[0, l]
        base = window(start, points, width)
        place = base + lax.broadcasted_iota(jnp.int32, (1, width), 1)
        inside = (place >= start) & (place < start + size)
        vec = jnp.where(inside, sorted_ref[:, pl.ds(base, width)], 0.0).astype(bf16)
        scr[pl.ds(l, rank, stride=leaves), :] = dot(basis_ref[:, pl.ds(base, width)], vec, NT)
        start = start + size
    coeff_ref[...] = scr[...].astype(bf16)


def up_root_kernel(
    self_id, partner, coeff_ref, leaf_ref, mid_ref, root_ref, dev_ref, group_ref, msg_ref, scr, dev_scr
):
    rank = 32
    vecs = coeff_ref.shape[1]
    leaves = leaf_ref.shape[0]
    middle = mid_ref.shape[0]
    slots = dev_ref.shape[0]
    subtrees = msg_ref.shape[0]
    groups = group_ref.shape[0]
    lanes = middle * vecs
    maps = spread(leaf_ref, rank)
    coeff = jnp.concatenate([coeff_ref[...].astype(f32)] * middle, axis=1)
    rows = lax.broadcasted_iota(jnp.int32, (rank * leaves, lanes), 0)
    cols = lax.broadcasted_iota(jnp.int32, (rank * leaves, lanes), 1)
    mine = (rows % leaves) // 8 == cols // vecs
    coeff = jnp.where(mine, coeff, 0.0).astype(bf16)
    mid = dot(coeff, maps, TN).astype(bf16)
    spread_into(scr, mid_ref, 0, 8, rank)
    spread_into(scr, root_ref, middle, 8, rank)
    spread_into(dev_scr, dev_ref, 0, slots, rank)
    root = jnp.zeros((vecs, rank), f32)
    for m in range(middle):
        block = scr[pl.ds(m, rank, stride=8), :][:, :rank].astype(bf16)
        root = root + dot(mid[m * vecs : (m + 1) * vecs], block, NN)
    root = root.astype(bf16)
    term = dot(root, scr[pl.ds(middle, rank, stride=8), :][:, :rank].astype(bf16), NN)
    blank = jnp.zeros((vecs, rank), f32)
    for g in range(groups):
        chunk = group_ref[g : g + 1, :]
        part = jnp.concatenate(
            [chunk[:, h * rank : (h + 1) * rank] for h in range(4)]
            + [jnp.zeros((vecs - 4, rank), f32)],
            axis=0,
        )
        tile = jnp.concatenate([root.astype(f32), term, blank, part], axis=1).astype(bf16)
        for d in range(8):
            msg_ref[g * 8 + d] = tile
    for c in range(slots):
        who = partner[0, c]
        live = who >= 0
        where = jnp.where(live, who, self_id[0])
        block = dev_scr[pl.ds(c, rank, stride=slots), :][:, :rank].astype(bf16)
        back = dot(root, block, NN)
        back = jnp.where(live, back, 0.0).astype(bf16)
        msg_ref[where, :, 2 * rank : 3 * rank] = back


def down_kernel(
    sizes,
    partner,
    got_ref,
    morton_ref,
    basis_ref,
    leaf_ref,
    mid_ref,
    root_ref,
    dev_ref,
    near_ref,
    out_ref,
    got,
    scr,
    dev_scr,
    total_scr,
    sorted_ref,
):
    rank, points = basis_ref.shape
    subtrees, vecs, tile_lanes = got_ref.shape
    leaves = leaf_ref.shape[0]
    middle = mid_ref.shape[0]
    slots = dev_ref.shape[0]
    groups = subtrees // 8
    highs = points // SPLIT
    width = min(points, LEAF + 128)
    got[...] = got_ref[...].astype(f32).reshape(subtrees * vecs, tile_lanes)
    spread_into(scr, mid_ref, 0, 8, rank)
    spread_into(scr, root_ref, middle, 8, rank)
    spread_into(dev_scr, dev_ref, 0, slots, rank)
    back = jnp.zeros((vecs, rank), f32)
    far = jnp.zeros((vecs, rank), f32)
    for g in range(groups):
        total = got[g * 8 * vecs : (g * 8 + 1) * vecs, :]
        for d in range(1, 8):
            total = total + got[(g * 8 + d) * vecs : (g * 8 + d + 1) * vecs, :]
        back = back + total[:, 2 * rank : 3 * rank]
        group = total[:, rank : 2 * rank].astype(bf16)
        pitch = groups // 4
        block = got[pl.ds(g // 4 * vecs + g % 4, rank, stride=pitch * vecs), :]
        far = far + dot(group, block[:, 3 * rank : 4 * rank].astype(bf16), NT)
    total = back
    for c in range(slots):
        who = partner[0, c]
        live = who >= 0
        other = got_ref[jnp.maximum(who, 0)][:, :rank].astype(f32)
        other = jnp.where(live, other, 0.0).astype(bf16)
        block = dev_scr[pl.ds(c, rank, stride=slots), :][:, :rank].astype(bf16)
        total = total + dot(other, block, NT)
    root_map = scr[pl.ds(middle, rank, stride=8), :][:, :rank].astype(bf16)
    total = (total + dot(far.astype(bf16), root_map, NT)).astype(bf16)
    mids = []
    for m in range(middle):
        block = scr[pl.ds(m, rank, stride=8), :][:, :rank].astype(bf16)
        mids.append(dot(total, block, NT))
    mids = jnp.concatenate(mids, axis=0).astype(bf16)
    maps = spread(leaf_ref, rank)
    down = dot(maps, mids, NT)
    rows = lax.broadcasted_iota(jnp.int32, (rank * leaves, 1), 0)
    mine = (rows % leaves) // 8
    leaf = near_ref[...]
    for m in range(middle):
        leaf = leaf + jnp.where(mine == m, down[:, m * vecs : (m + 1) * vecs], 0.0)
    total_scr[...] = leaf
    start = jnp.int32(0)
    for l in range(leaves):
        size = sizes[0, l]
        base = window(start, points, width)
        place = base + lax.broadcasted_iota(jnp.int32, (1, width), 1)
        inside = (place >= start) & (place < start + size)
        leaf = total_scr[pl.ds(l, rank, stride=leaves), :].astype(bf16)
        value = dot(leaf, basis_ref[:, pl.ds(base, width)], TN)
        old = sorted_ref[:, pl.ds(base, width)]
        sorted_ref[:, pl.ds(base, width)] = jnp.where(inside, value, old)
        start = start + size
    step = 256
    result = jnp.zeros((highs * vecs, SPLIT), f32)
    for k in range(points // step):
        morton = morton_ref[:, k * step : (k + 1) * step]
        high = morton // SPLIT
        value = sorted_ref[:, k * step : (k + 1) * step]
        masked = jnp.concatenate([jnp.where(high == h, value, 0.0) for h in range(highs)], axis=0)
        result = result + dot(masked.astype(bf16), one_hot_low(morton, step), NT)
    for h in range(highs):
        out_ref[:, h * SPLIT : (h + 1) * SPLIT] = result[h * vecs : (h + 1) * vecs]


smem = pl.BlockSpec(memory_space=pltpu.SMEM)
vmem = pl.BlockSpec(memory_space=pltpu.VMEM)


def body(
    vectors,
    morton_order,
    leaf_sizes,
    leaf_basis,
    leaf_transfer,
    mid_transfer,
    root_transfer,
    leaf_pairs,
    leaf_coupling,
    dev_partner,
    dev_coupling,
    grp_partner,
    grp_coupling,
):
    rank, points = leaf_basis.shape
    vecs = vectors.shape[0]
    leaves = leaf_sizes.shape[1]
    middle = mid_transfer.shape[0]
    row_width = rank * vecs
    slots = dev_coupling.shape[0]
    subtrees = lax.axis_size("leaf")
    groups = subtrees // 8
    self_id = lax.axis_index("leaf").astype(jnp.int32)
    own_group = self_id // 8

    group_ids = jnp.arange(groups, dtype=jnp.int32)
    hot = (grp_partner[0][:, None] == group_ids[None, :]).astype(bf16)
    by_partner = jnp.einsum(
        "sh,sx->hx", hot, grp_coupling, preferred_element_type=f32
    ).reshape(groups, rank, rank)
    self_hot = (group_ids == own_group).astype(f32)
    parts = (
        self_hot[:, None, None, None] * by_partner.transpose(1, 0, 2)[None]
        + self_hot[None, None, :, None] * by_partner.transpose(0, 2, 1)[:, :, None, :]
    )
    parts = parts.astype(bf16).reshape(groups, subtrees, 4 * rank).transpose(1, 0, 2)
    chunks = lax.all_to_all(parts, "leaf", 0, 0, tiled=True)

    coeff = pl.pallas_call(
        up_leaf_kernel,
        out_shape=jax.ShapeDtypeStruct((rank * leaves, vecs), bf16),
        in_specs=[smem, vmem, vmem, vmem],
        out_specs=vmem,
        scratch_shapes=[pltpu.VMEM((vecs, points), f32), pltpu.VMEM((rank * leaves, vecs), f32)],
        name="up_leaf",
    )(leaf_sizes, vectors, morton_order, leaf_basis)

    chunk = chunks.astype(f32).sum(0)
    message = pl.pallas_call(
        up_root_kernel,
        out_shape=jax.ShapeDtypeStruct((subtrees, vecs, 4 * rank), bf16),
        in_specs=[smem, smem] + [vmem] * 6,
        out_specs=vmem,
        scratch_shapes=[
            pltpu.VMEM((rank * 8, rank), f32),
            pltpu.VMEM((rank * slots, rank), f32),
        ],
        name="up_root",
    )(
        self_id[None],
        dev_partner,
        coeff,
        leaf_transfer,
        mid_transfer,
        root_transfer,
        dev_coupling,
        chunk,
    )
    got = lax.all_to_all(message, "leaf", 0, 0, tiled=True)

    leaf_blocks = leaf_coupling.reshape(-1, rank, rank)
    leaf_ids = jnp.arange(leaves, dtype=jnp.int32)
    first_hot = (leaf_pairs[0][:, None] == leaf_ids[None, :]).astype(bf16)
    second_hot = (leaf_pairs[1][:, None] == leaf_ids[None, :]).astype(bf16)
    flat = coeff.reshape(rank, leaves, vecs).transpose(1, 0, 2).reshape(leaves, row_width)
    from_second = jnp.dot(second_hot, flat, preferred_element_type=f32).astype(bf16)
    from_first = jnp.dot(first_hot, flat, preferred_element_type=f32).astype(bf16)
    forward = jnp.einsum(
        "pij,pjv->piv", leaf_blocks, from_second.reshape(-1, rank, vecs), preferred_element_type=f32
    )
    backward = jnp.einsum(
        "pij,piv->pjv", leaf_blocks, from_first.reshape(-1, rank, vecs), preferred_element_type=f32
    )
    near = jnp.dot(first_hot.T, forward.reshape(-1, row_width).astype(bf16), preferred_element_type=f32)
    near = near + jnp.dot(
        second_hot.T, backward.reshape(-1, row_width).astype(bf16), preferred_element_type=f32
    )
    near = near.reshape(leaves, rank, vecs).transpose(1, 0, 2).reshape(rank * leaves, vecs)

    return pl.pallas_call(
        down_kernel,
        out_shape=jax.ShapeDtypeStruct((vecs, points), f32),
        in_specs=[smem, smem] + [vmem] * 8,
        out_specs=vmem,
        scratch_shapes=[
            pltpu.VMEM((subtrees * vecs, 4 * rank), f32),
            pltpu.VMEM((rank * 8, rank), f32),
            pltpu.VMEM((rank * slots, rank), f32),
            pltpu.VMEM((rank * leaves, vecs), f32),
            pltpu.VMEM((vecs, points), f32),
        ],
        name="down",
    )(
        leaf_sizes,
        dev_partner,
        got,
        morton_order,
        leaf_basis,
        leaf_transfer,
        mid_transfer,
        root_transfer,
        dev_coupling,
        near,
    )


def solution(mesh):
    in_specs = (
        P(None, "leaf"),
        P("leaf", None),
        P("leaf", None),
        P(None, "leaf"),
        P("leaf", None),
        P("leaf", None),
        P("leaf", None),
        P(None, "leaf"),
        P("leaf", None),
        P("leaf", None),
        P("leaf", None),
        P("leaf", None),
        P("leaf", None),
    )
    out_specs = P(None, "leaf")
    return jax.shard_map(body, mesh=mesh, in_specs=in_specs, out_specs=out_specs, check_vma=False)
```

```python
import functools

import jax
import jax.numpy as jnp
from jax import lax
from jax.experimental import pallas as pl
from jax.experimental.pallas import tpu as pltpu
from jax.sharding import PartitionSpec as P

LEAF = 256
SPLIT = 256

bf16 = jnp.bfloat16
f32 = jnp.float32


def dot(a, b, over):
    return lax.dot_general(a, b, (over, ((), ())), preferred_element_type=f32)


NN = ((1,), (0,))
NT = ((1,), (1,))
TN = ((0,), (0,))


def one_hot_low(morton, width):
    rows = lax.broadcasted_iota(jnp.int32, (SPLIT, width), 0)
    return jnp.where(rows == (morton & (SPLIT - 1)), 1.0, 0.0).astype(bf16)


def window(start, points, width):
    base = jnp.minimum(start // 128 * 128, points - width)
    return pl.multiple_of(base, 128)


def spread(scr, ref, row, pitch, rank):
    flat = ref[...].astype(f32)
    n = flat.shape[0]
    for i in range(rank):
        scr[i * pitch + row : i * pitch + row + n, :rank] = flat[:, rank * i : rank * (i + 1)]


def block_of(scr, n, pitch, rank):
    return scr[pl.ds(n, rank, stride=pitch), :][:, :rank].astype(bf16)


def beside(tiles):
    return jnp.concatenate(tiles, axis=1)


def up_kernel(
    self_id,
    sizes,
    partner,
    vec_ref,
    morton_ref,
    basis_ref,
    leaf_ref,
    mid_ref,
    root_ref,
    dev_ref,
    *rest,
    few,
):
    group_refs, (coeff_ref, msg_ref, sorted_ref, leaf_scr, scr, dev_scr, group_scr) = (
        rest[:-7],
        rest[-7:],
    )
    vecs, points = vec_ref.shape
    rank = basis_ref.shape[0]
    leaves = sizes.shape[1]
    middle = mid_ref.shape[0]
    slots = dev_ref.shape[0]
    subtrees = msg_ref.shape[0]
    groups = subtrees // 8
    highs = points // SPLIT
    width = min(points, LEAF + 128)
    stacked = jnp.concatenate(
        [vec_ref[:, h * SPLIT : (h + 1) * SPLIT].astype(bf16) for h in range(highs)], axis=0
    )
    step = 256
    for k in range(points // step):
        morton = morton_ref[:, k * step : (k + 1) * step]
        mixed = dot(stacked, one_hot_low(morton, step), NN)
        high = morton // SPLIT
        picked = jnp.zeros((vecs, step), f32)
        for h in range(highs):
            picked = picked + jnp.where(high == h, mixed[h * vecs : (h + 1) * vecs], 0.0)
        sorted_ref[:, k * step : (k + 1) * step] = picked
    spread(leaf_scr, leaf_ref, 0, leaves, rank)
    spread(scr, mid_ref, 0, 8, rank)
    spread(scr, root_ref, middle, 8, rank)
    spread(dev_scr, dev_ref, 0, slots, rank)
    start = jnp.int32(0)
    mids = [jnp.zeros((vecs, rank), f32) for _ in range(middle)]
    for l in range(leaves):
        size = sizes[0, l]
        base = window(start, points, width)
        place = base + lax.broadcasted_iota(jnp.int32, (1, width), 1)
        inside = (place >= start) & (place < start + size)
        vec = jnp.where(inside, sorted_ref[:, pl.ds(base, width)], 0.0).astype(bf16)
        coeff = dot(vec, basis_ref[:, pl.ds(base, width)], NT).astype(bf16)
        coeff_ref[l] = coeff
        mids[l // 8] = mids[l // 8] + dot(coeff, block_of(leaf_scr, l, leaves, rank), NN)
        start = start + size
    root = jnp.zeros((vecs, rank), f32)
    for m in range(middle):
        root = root + dot(mids[m].astype(bf16), block_of(scr, m, 8, rank), NN)
    root = root.astype(bf16)
    term = dot(root, block_of(scr, middle, 8, rank), NN)
    blank = jnp.zeros((vecs, rank), f32)
    own = self_id[0] // 8
    if few:
        spread(group_scr, group_refs[0], 0, 8, rank)
        spread(group_scr, group_refs[1], groups, 8, rank)
        half = rank // 2
        first = self_id[0] % 2 * (half * 8)

        def half_of(h):
            mine = group_scr[pl.ds(first + h, half, stride=8), :]
            other = group_scr[pl.ds(first + groups + h, half, stride=8), :]
            return (mine + other)[:, :rank]

        below = [half_of((own + 1 + q) % groups) for q in range(1, groups - 1)]
        below = beside([part for b in below for part in (b[:8], b[8:])])
    for g in range(groups):
        if few:
            part = half_of(jnp.where(own == g, (own + 1) % groups, g))
        else:
            chunk = group_refs[0][g : g + 1, :]
            part = jnp.concatenate(
                [chunk[:, h * rank : (h + 1) * rank] for h in range(4)]
                + [jnp.zeros((vecs - 4, rank), f32)],
                axis=0,
            )
        tile = beside([root.astype(f32), term, blank, part]).astype(bf16)
        if few:
            tile = jnp.concatenate([tile, below.astype(bf16)], axis=0)
        for d in range(8):
            msg_ref[g * 8 + d] = tile
    for c in range(slots):
        who = partner[0, c]
        live = who >= 0
        where = jnp.where(live, who, self_id[0])
        back = dot(root, block_of(dev_scr, c, slots, rank), NN)
        back = jnp.where(live, back, 0.0).astype(bf16)
        msg_ref[where, :vecs, 2 * rank : 3 * rank] = back


def near_kernel(
    sizes,
    pairs,
    coeff_ref,
    morton_ref,
    basis_ref,
    leaf_ref,
    mid_ref,
    root_ref,
    dev_ref,
    couple_ref,
    reach_ref,
    near_ref,
    dev_out,
    root_out,
    leaf_scr,
    scr,
    dev_scr,
    couple_scr,
    far_scr,
    sorted_ref,
):
    rank, points = basis_ref.shape
    leaves, vecs, _ = coeff_ref.shape
    middle = mid_ref.shape[0]
    slots = dev_ref.shape[0]
    npairs = couple_ref.shape[0]
    highs = points // SPLIT
    width = min(points, LEAF + 128)
    rows = rank + vecs
    spread(leaf_scr, leaf_ref, 0, leaves, rank)
    spread(scr, mid_ref, 0, 8, rank)
    spread(scr, root_ref, middle, 8, rank)
    spread(dev_scr, dev_ref, 0, slots, rank)
    spread(couple_scr, couple_ref, 0, npairs, rank)
    dev_out[...] = beside(
        [dev_scr[pl.ds(c, rank, stride=slots), :][:, :rank] for c in range(slots)]
    ).astype(bf16)
    root_out[...] = block_of(scr, middle, 8, rank)
    far_scr[...] = jnp.zeros_like(far_scr)
    for p in range(npairs):
        a = pairs[0, p]
        b = pairs[1, p]
        block = block_of(couple_scr, p, npairs, rank)
        to_a = dot(coeff_ref[b], block, NT)
        to_b = dot(coeff_ref[a], block, NN)
        far_scr[a] += to_a
        far_scr[b] += to_b
    start = jnp.int32(0)
    for l in range(leaves):
        size = sizes[0, l]
        base = window(start, points, width)
        place = base + lax.broadcasted_iota(jnp.int32, (1, width), 1)
        inside = (place >= start) & (place < start + size)
        reach = lax.dot_general(
            block_of(scr, l // 8, 8, rank),
            block_of(leaf_scr, l, leaves, rank),
            (((0,), (1,)), ((), ())),
            preferred_element_type=f32,
        )
        both = jnp.concatenate([reach, far_scr[l]], axis=0).astype(bf16)
        value = dot(both, basis_ref[:, pl.ds(base, width)], NN)
        old = sorted_ref[:, pl.ds(base, width)]
        sorted_ref[:, pl.ds(base, width)] = jnp.where(inside, value, old)
        start = start + size
    step = 256
    result = jnp.zeros((highs * rows, SPLIT), f32)
    for k in range(points // step):
        morton = morton_ref[:, k * step : (k + 1) * step]
        high = morton // SPLIT
        value = sorted_ref[:, k * step : (k + 1) * step]
        masked = jnp.concatenate([jnp.where(high == h, value, 0.0) for h in range(highs)], axis=0)
        result = result + dot(masked.astype(bf16), one_hot_low(morton, step), NT)
    for h in range(highs):
        reach_ref[:, h * SPLIT : (h + 1) * SPLIT] = result[h * rows : h * rows + rank].astype(bf16)
        near_ref[:, h * SPLIT : (h + 1) * SPLIT] = result[h * rows + rank : (h + 1) * rows]


def last_kernel(self_id, partner, got_ref, dev_ref, root_ref, reach_ref, near_ref, out_ref, got, group_scr, *, few):
    rank = root_ref.shape[0]
    subtrees, tall, tile_lanes = got_ref.shape
    vecs = near_ref.shape[0]
    slots = dev_ref.shape[1] // rank
    groups = subtrees // 8
    own = self_id[0] // 8
    chosen = []
    for c in range(slots):
        who = partner[0, c]
        other = got_ref[jnp.maximum(who, 0)][:vecs, :rank].astype(f32)
        chosen.append(jnp.where(who >= 0, other, 0.0))
    total = dot(beside(chosen).astype(bf16), dev_ref[...], NT)
    if not few:
        got[...] = got_ref[...].astype(f32).reshape(subtrees * tall, tile_lanes)
    far = jnp.zeros((vecs, rank), f32)
    for g in range(groups):
        level = got_ref[g * 8, :vecs].astype(f32)
        for d in range(1, 8):
            level = level + got_ref[g * 8 + d, :vecs].astype(f32)
        total = total + level[:, 2 * rank : 3 * rank]
        group = level[:, rank : 2 * rank]
        if few:
            group_scr[g] = group
        else:
            pitch = groups // 4
            block = got[pl.ds(g // 4 * vecs + g % 4, rank, stride=pitch * vecs), :]
            far = far + dot(group.astype(bf16), block[:, 3 * rank : 4 * rank].astype(bf16), NT)
    if few:

        def stack_of(g, q):
            halves = []
            for core in range(2):
                acc = 0.0
                for chip in range(4):
                    message = got_ref.at[g * 8 + 2 * chip + core]
                    if q == 0:
                        part = message[:vecs, 3 * rank :].astype(f32)
                    else:
                        part = message[vecs:, (q - 1) * 2 * rank : q * 2 * rank].astype(f32)
                    acc = acc + part
                halves.append(acc if q == 0 else jnp.concatenate([acc[:, :rank], acc[:, rank:]], axis=0))
            return jnp.concatenate(halves, axis=0).astype(bf16)

        for q in range(groups - 1):
            other = (own + 1 + q) % groups
            group = group_scr[other].astype(bf16)
            far = far + dot(group, stack_of(own, q), NT) + dot(group, stack_of(other, 0), NN)
    total = (total + dot(far.astype(bf16), root_ref[...], NT)).astype(bf16)
    out_ref[...] = near_ref[...] + dot(total, reach_ref[...], NN)


smem = pl.BlockSpec(memory_space=pltpu.SMEM)
vmem = pl.BlockSpec(memory_space=pltpu.VMEM)


def body(
    vectors,
    morton_order,
    leaf_sizes,
    leaf_basis,
    leaf_transfer,
    mid_transfer,
    root_transfer,
    leaf_pairs,
    leaf_coupling,
    dev_partner,
    dev_coupling,
    grp_partner,
    grp_coupling,
):
    rank, points = leaf_basis.shape
    vecs = vectors.shape[0]
    leaves = leaf_sizes.shape[1]
    slots = dev_coupling.shape[0]
    npairs = leaf_coupling.shape[0]
    subtrees = lax.axis_size("leaf")
    groups = subtrees // 8
    few = groups == 4
    self_id = lax.axis_index("leaf").astype(jnp.int32)
    own_group = self_id // 8
    group_ids = jnp.arange(groups, dtype=jnp.int32)
    hot = (grp_partner[0][:, None] == group_ids[None, :]).astype(bf16)
    by_partner = jnp.einsum("sh,sx->hx", hot, grp_coupling, preferred_element_type=f32)
    if few:
        by_partner = by_partner.astype(bf16)
        swap = [(d, d ^ 1) for d in range(subtrees)]
        group_args = (by_partner, lax.ppermute(by_partner, "leaf", swap))
        tall = vecs + 8
    else:
        by_partner = by_partner.reshape(groups, rank, rank)
        self_hot = (group_ids == own_group).astype(f32)
        parts = (
            self_hot[:, None, None, None] * by_partner.transpose(1, 0, 2)[None]
            + self_hot[None, None, :, None] * by_partner.transpose(0, 2, 1)[:, :, None, :]
        )
        parts = parts.astype(bf16).reshape(groups, subtrees, 4 * rank).transpose(1, 0, 2)
        chunks = lax.all_to_all(parts, "leaf", 0, 0, tiled=True)
        group_args = (chunks.astype(f32).sum(0),)
        tall = vecs

    coeff, message = pl.pallas_call(
        functools.partial(up_kernel, few=few),
        out_shape=(
            jax.ShapeDtypeStruct((leaves, vecs, rank), bf16),
            jax.ShapeDtypeStruct((subtrees, tall, 4 * rank), bf16),
        ),
        in_specs=[smem] * 3 + [vmem] * (7 + len(group_args)),
        out_specs=(vmem, vmem),
        scratch_shapes=[
            pltpu.VMEM((vecs, points), f32),
            pltpu.VMEM((rank * leaves, rank), f32),
            pltpu.VMEM((rank * 8, rank), f32),
            pltpu.VMEM((rank * slots, rank), f32),
            pltpu.VMEM((rank * 8, rank), f32),
        ],
        name="up",
    )(
        self_id[None],
        leaf_sizes,
        dev_partner,
        vectors,
        morton_order,
        leaf_basis,
        leaf_transfer,
        mid_transfer,
        root_transfer,
        dev_coupling,
        *group_args,
    )
    got = lax.all_to_all(message, "leaf", 0, 0, tiled=True)

    reach, near, dev_wide, root_map = pl.pallas_call(
        near_kernel,
        out_shape=(
            jax.ShapeDtypeStruct((rank, points), bf16),
            jax.ShapeDtypeStruct((vecs, points), f32),
            jax.ShapeDtypeStruct((rank, slots * rank), bf16),
            jax.ShapeDtypeStruct((rank, rank), bf16),
        ),
        in_specs=[smem] * 2 + [vmem] * 8,
        out_specs=(vmem,) * 4,
        scratch_shapes=[
            pltpu.VMEM((rank * leaves, rank), f32),
            pltpu.VMEM((rank * 8, rank), f32),
            pltpu.VMEM((rank * slots, rank), f32),
            pltpu.VMEM((rank * npairs, rank), f32),
            pltpu.VMEM((leaves, vecs, rank), f32),
            pltpu.VMEM((rank + vecs, points), f32),
        ],
        cost_estimate=pl.CostEstimate(flops=4 << 30, bytes_accessed=4 << 20, transcendentals=0),
        name="near",
    )(
        leaf_sizes,
        leaf_pairs,
        coeff,
        morton_order,
        leaf_basis,
        leaf_transfer,
        mid_transfer,
        root_transfer,
        dev_coupling,
        leaf_coupling,
    )

    return pl.pallas_call(
        functools.partial(last_kernel, few=few),
        out_shape=jax.ShapeDtypeStruct((vecs, points), f32),
        in_specs=[smem] * 2 + [vmem] * 5,
        out_specs=vmem,
        scratch_shapes=[
            pltpu.VMEM((8 if few else subtrees * tall, 4 * rank), f32),
            pltpu.VMEM((groups, vecs, rank), f32),
        ],
        name="last",
    )(self_id[None], dev_partner, got, dev_wide, root_map, reach, near)


def solution(mesh):
    in_specs = (
        P(None, "leaf"),
        P("leaf", None),
        P("leaf", None),
        P(None, "leaf"),
        P("leaf", None),
        P("leaf", None),
        P("leaf", None),
        P(None, "leaf"),
        P("leaf", None),
        P("leaf", None),
        P("leaf", None),
        P("leaf", None),
        P("leaf", None),
    )
    out_specs = P(None, "leaf")
    return jax.shard_map(body, mesh=mesh, in_specs=in_specs, out_specs=out_specs, check_vma=False)
```

```python
import functools

import jax
import jax.numpy as jnp
from jax import lax
from jax.experimental import pallas as pl
from jax.experimental.pallas import tpu as pltpu
from jax.sharding import PartitionSpec as P

LEAF = 256
SPLIT = 256

bf16 = jnp.bfloat16
f32 = jnp.float32


def dot(a, b, over):
    return lax.dot_general(a, b, (over, ((), ())), preferred_element_type=f32)


NN = ((1,), (0,))
NT = ((1,), (1,))
TN = ((0,), (0,))


def one_hot_low(morton, width):
    rows = lax.broadcasted_iota(jnp.int32, (SPLIT, width), 0).astype(bf16)
    low = (morton & (SPLIT - 1)).astype(f32).astype(bf16)
    return jnp.where(rows == low, jnp.ones((), bf16), jnp.zeros((), bf16))


def window(start, points, width):
    base = jnp.minimum(start - (start & 127), points - width)
    return pl.multiple_of(base, 128)


def inside_of(start, size, base, shape):
    place = lax.broadcasted_iota(jnp.int32, shape, 1) + (base - start)
    return place.astype(jnp.uint32) < size.astype(jnp.uint32)


def pitch_of(n):
    return n + 8 if n % 16 == 0 else n


def spread(scr, ref, row, pitch, rank):
    flat = ref[...].astype(f32)
    n = flat.shape[0]
    for i in range(rank):
        scr[i * pitch + row : i * pitch + row + n, :rank] = flat[:, rank * i : rank * (i + 1)]


def block_of(scr, n, pitch, rank):
    return scr[pl.ds(n, rank, stride=pitch), :][:, :rank].astype(bf16)


def beside(tiles):
    return jnp.concatenate(tiles, axis=1)


def up_kernel(
    sizes_hbm,
    partner_hbm,
    vec_hbm,
    morton_hbm,
    basis_hbm,
    leaf_hbm,
    mid_hbm,
    root_hbm,
    dev_hbm,
    who_hbm,
    group_hbm,
    coeff_ref,
    tops_ref,
    back_ref,
    who_ref,
    group_ref,
    sizes,
    partner,
    vec_ref,
    morton_ref,
    basis_ref,
    leaf_ref,
    mid_ref,
    root_ref,
    dev_ref,
    sems,
    sorted_ref,
    leaf_scr,
    scr,
    dev_scr,
):
    vecs, points = vec_ref.shape
    rank = basis_ref.shape[0]
    leaves = sizes.shape[1]
    middle = mid_ref.shape[0]
    slots = dev_ref.shape[0]
    highs = points // SPLIT
    width = min(points, LEAF + 128)
    copies = [
        pltpu.make_async_copy(src, dst, sems.at[n])
        for n, (src, dst) in enumerate(
            (
                (morton_hbm, morton_ref),
                (vec_hbm, vec_ref),
                (basis_hbm, basis_ref),
                (leaf_hbm, leaf_ref),
                (mid_hbm, mid_ref),
                (root_hbm, root_ref),
                (dev_hbm, dev_ref),
                (sizes_hbm, sizes),
                (partner_hbm, partner),
                (who_hbm, who_ref),
                (group_hbm, group_ref),
            )
        )
    ]
    for copy in copies:
        copy.start()
    copies[0].wait()
    copies[1].wait()
    stacked = jnp.concatenate(
        [vec_ref[:, h * SPLIT : (h + 1) * SPLIT].astype(bf16) for h in range(highs)], axis=0
    )
    step = 256
    for k in range(points // step):
        morton = morton_ref[:, k * step : (k + 1) * step]
        mixed = dot(stacked, one_hot_low(morton, step), NN)
        high = morton // SPLIT
        picked = mixed[:vecs]
        for h in range(1, highs):
            picked = jnp.where(high == h, mixed[h * vecs : (h + 1) * vecs], picked)
        sorted_ref[:, k * step : (k + 1) * step] = picked
    for copy in copies[2:]:
        copy.wait()
    spread(leaf_scr, leaf_ref, 0, pitch_of(leaves), rank)
    spread(scr, mid_ref, 0, 8, rank)
    spread(scr, root_ref, middle, 8, rank)
    spread(dev_scr, dev_ref, 0, pitch_of(slots), rank)
    back_ref[...] = jnp.zeros_like(back_ref)
    start = jnp.int32(0)
    coeffs = []
    for l in range(leaves):
        size = sizes[0, l]
        base = window(start, points, width)
        inside = inside_of(start, size, base, (vecs, width))
        vec = jnp.where(inside, sorted_ref[:, pl.ds(base, width)], 0.0).astype(bf16)
        coeff = dot(vec, basis_ref[:, pl.ds(base, width)], NT)
        coeff_ref[l] = coeff.astype(bf16)
        coeffs.append(coeff)
        start = start + size
    mids = []
    for m in range(middle):
        kids = range(8 * m, 8 * m + 8)
        maps = [block_of(leaf_scr, l, pitch_of(leaves), rank) for l in kids]
        maps = jnp.concatenate(maps, axis=0)
        mids.append(dot(beside([coeffs[l] for l in kids]).astype(bf16), maps, NN))
    maps = jnp.concatenate([block_of(scr, m, 8, rank) for m in range(middle)], axis=0)
    root = dot(beside(mids).astype(bf16), maps, NN).astype(bf16)
    term = dot(root, block_of(scr, middle, 8, rank), NN)
    tops_ref[...] = beside([root.astype(f32), term])
    self_id = lax.axis_index("leaf")
    for c in range(slots):
        who = partner[0, c]
        back = dot(root, block_of(dev_scr, c, pitch_of(slots), rank), NN)
        back_ref[jnp.where(who >= 0, who, self_id)] = jnp.where(who >= 0, back, 0.0)


def pack_kernel(tops_ref, back_ref, *rest, few):
    group_refs, (msg_hbm, msg_ref, group_scr, half_scr, sems) = rest[:-5], rest[-5:]
    vecs = tops_ref.shape[0]
    rank = tops_ref.shape[1] // 2
    subtrees = msg_ref.shape[0]
    groups = subtrees // 8
    self_id = lax.axis_index("leaf")
    own = self_id // 8
    copies = []
    if few:
        held = group_refs[2].shape[0]
        pitch = 2 * held
        spread(group_scr, group_refs[2], 0, pitch, rank)
        spread(group_scr, group_refs[3], held, pitch, rank)
        half = rank // 2
        first = self_id % 2 * (half * pitch)
        sums = [jnp.zeros((half, rank), f32) for _ in range(groups)]
        for s in range(pitch):
            target = group_refs[s // held][:, s % held : s % held + 1]
            block = group_scr[pl.ds(first + s, half, stride=pitch), :][:, :rank]
            for h in range(groups):
                sums[h] = sums[h] + jnp.where(target == h, block, 0.0)
        for h in range(groups):
            half_scr[h] = sums[h]
        below = [half_scr[(own + 1 + q) % groups] for q in range(1, groups - 1)]
        below = beside([part for b in below for part in (b[:8], b[8:])]).astype(bf16)
    blank = jnp.zeros((vecs, rank), f32)
    for g in range(groups):
        if few:
            part = half_scr[jnp.where(own == g, (own + 1) % groups, g)]
        else:
            chunk = group_refs[0][g : g + 1, :]
            part = jnp.concatenate(
                [chunk[:, h * rank : (h + 1) * rank] for h in range(4)]
                + [jnp.zeros((vecs - 4, rank), f32)],
                axis=0,
            )
        tile = beside([tops_ref[...], blank, part]).astype(bf16)
        if few:
            tile = jnp.concatenate([tile, below], axis=0)
        for d in range(8 * g, 8 * g + 8):
            msg_ref[d] = tile
            msg_ref[d, :vecs, 2 * rank : 3 * rank] = back_ref[d].astype(bf16)
        some = pl.ds(8 * g, 8)
        copies.append(pltpu.make_async_copy(msg_ref.at[some], msg_hbm.at[some], sems.at[g]))
        copies[-1].start()
    for copy in copies:
        copy.wait()


def near_kernel(
    sizes,
    pairs,
    partner,
    coeff_ref,
    morton_ref,
    basis_ref,
    leaf_ref,
    mid_ref,
    root_ref,
    dev_ref,
    couple_ref,
    reach_ref,
    near_ref,
    dev_out,
    root_out,
    leaf_scr,
    scr,
    dev_scr,
    couple_scr,
    far_scr,
    sorted_ref,
    wide_scr,
):
    rank, points = basis_ref.shape
    leaves, vecs, _ = coeff_ref.shape
    middle = mid_ref.shape[0]
    slots = dev_ref.shape[0]
    npairs = couple_ref.shape[0]
    highs = points // SPLIT
    width = min(points, LEAF + 128)
    rows = rank + vecs
    spread(leaf_scr, leaf_ref, 0, pitch_of(leaves), rank)
    spread(scr, mid_ref, 0, 8, rank)
    spread(scr, root_ref, middle, 8, rank)
    spread(dev_scr, dev_ref, 0, pitch_of(slots), rank)
    spread(couple_scr, couple_ref, 0, pitch_of(npairs), rank)
    same = lax.broadcasted_iota(jnp.int32, (rank, 4 * rank), 1)
    same = same == lax.broadcasted_iota(jnp.int32, (rank, 4 * rank), 0) + 2 * rank
    same = jnp.where(same, 1.0, 0.0)
    subtrees = wide_scr.shape[0] - 1
    for b in range(subtrees):
        wide_scr[b] = same
    for c in range(slots):
        who = partner[0, c]
        block = dev_scr[pl.ds(c, rank, stride=pitch_of(slots)), :][:, :rank]
        wide_scr[jnp.where(who >= 0, who, subtrees), :, :rank] = block
    for b in range(subtrees):
        dev_out[:, 4 * rank * b : 4 * rank * (b + 1)] = wide_scr[b].astype(bf16)
    root_out[...] = block_of(scr, middle, 8, rank)
    far_scr[...] = jnp.zeros_like(far_scr)
    for p in range(npairs):
        a = pairs[0, p]
        b = pairs[1, p]
        block = block_of(couple_scr, p, pitch_of(npairs), rank)
        to_a = dot(coeff_ref[b], block, NT)
        to_b = dot(coeff_ref[a], block, NN)
        far_scr[a] += to_a
        far_scr[b] += to_b
    start = jnp.int32(0)
    for l in range(leaves):
        size = sizes[0, l]
        base = window(start, points, width)
        inside = inside_of(start, size, base, (rows, width))
        reach = lax.dot_general(
            block_of(scr, l // 8, 8, rank),
            block_of(leaf_scr, l, pitch_of(leaves), rank),
            (((0,), (1,)), ((), ())),
            preferred_element_type=f32,
        )
        both = jnp.concatenate([reach, far_scr[l]], axis=0).astype(bf16)
        value = dot(both, basis_ref[:, pl.ds(base, width)], NN)
        old = sorted_ref[:, pl.ds(base, width)]
        sorted_ref[:, pl.ds(base, width)] = jnp.where(inside, value, old)
        start = start + size
    step = 256
    result = jnp.zeros((highs * rows, SPLIT), f32)
    for k in range(points // step):
        morton = morton_ref[:, k * step : (k + 1) * step]
        high = morton // SPLIT
        value = sorted_ref[:, k * step : (k + 1) * step]
        masked = jnp.concatenate([jnp.where(high == h, value, 0.0) for h in range(highs)], axis=0)
        result = result + dot(masked.astype(bf16), one_hot_low(morton, step), NT)
    for h in range(highs):
        reach_ref[:, h * SPLIT : (h + 1) * SPLIT] = result[h * rows : h * rows + rank].astype(bf16)
        near_ref[:, h * SPLIT : (h + 1) * SPLIT] = result[h * rows + rank : (h + 1) * rows]


def last_kernel(
    got_ref,
    dev_ref,
    root_ref,
    reach_ref,
    near_ref,
    out_hbm,
    got,
    group_scr,
    out_ref,
    sems,
    *,
    few,
):
    rank = root_ref.shape[0]
    subtrees, tall, tile_lanes = got_ref.shape
    vecs = near_ref.shape[0]
    groups = subtrees // 8
    own = lax.axis_index("leaf") // 8
    total = dot(beside([got_ref[b][:vecs] for b in range(subtrees)]), dev_ref[...], NT)
    if not few:
        got[...] = got_ref[...].astype(f32).reshape(subtrees * tall, tile_lanes)
    far = jnp.zeros((vecs, rank), f32)
    for g in range(groups):
        level = got_ref[g * 8, :vecs].astype(f32)
        for d in range(1, 8):
            level = level + got_ref[g * 8 + d, :vecs].astype(f32)
        group = level[:, rank : 2 * rank]
        if few:
            group_scr[g] = group
        else:
            pitch = groups // 4
            block = got[pl.ds(g // 4 * vecs + g % 4, rank, stride=pitch * vecs), :]
            far = far + dot(group.astype(bf16), block[:, 3 * rank : 4 * rank].astype(bf16), NT)
    if few:

        def stack_of(g, q):
            halves = []
            for core in range(2):
                acc = 0.0
                for chip in range(4):
                    message = got_ref.at[g * 8 + 2 * chip + core]
                    if q == 0:
                        part = message[:vecs, 3 * rank :].astype(f32)
                    else:
                        part = message[vecs:, (q - 1) * 2 * rank : q * 2 * rank].astype(f32)
                    acc = acc + part
                halves.append(acc if q == 0 else jnp.concatenate([acc[:, :rank], acc[:, rank:]], axis=0))
            return jnp.concatenate(halves, axis=0).astype(bf16)

        for q in range(groups - 1):
            other = (own + 1 + q) % groups
            group = group_scr[other].astype(bf16)
            far = far + dot(group, stack_of(own, q), NT) + dot(group, stack_of(other, 0), NN)
    total = (total + dot(far.astype(bf16), root_ref[...], NT)).astype(bf16)
    points = near_ref.shape[1]
    pieces = sems.shape[0]
    copies = []
    for n in range(pieces):
        cols = pl.ds(n * (points // pieces), points // pieces)
        out_ref[:, cols] = near_ref[:, cols] + dot(total, reach_ref[:, cols], NN)
        copies.append(pltpu.make_async_copy(out_ref.at[:, cols], out_hbm.at[:, cols], sems.at[n]))
        copies[-1].start()
    for copy in copies:
        copy.wait()


smem = pl.BlockSpec(memory_space=pltpu.SMEM)
vmem = pl.BlockSpec(memory_space=pltpu.VMEM)


def on_chip(x):
    return pltpu.with_memory_space_constraint(x, pltpu.VMEM)


def body(
    vectors,
    morton_order,
    leaf_sizes,
    leaf_basis,
    leaf_transfer,
    mid_transfer,
    root_transfer,
    leaf_pairs,
    leaf_coupling,
    dev_partner,
    dev_coupling,
    grp_partner,
    grp_coupling,
):
    rank, points = leaf_basis.shape
    vecs = vectors.shape[0]
    leaves = leaf_sizes.shape[1]
    slots = dev_coupling.shape[0]
    npairs = leaf_coupling.shape[0]
    subtrees = lax.axis_size("leaf")
    groups = subtrees // 8
    few = groups == 4
    keep, made = (on_chip, pltpu.VMEM) if few else (lambda x: x, jax.ShapeDtypeStruct)
    self_id = lax.axis_index("leaf").astype(jnp.int32)
    own_group = self_id // 8
    group_ids = jnp.arange(groups, dtype=jnp.int32)
    if few:
        swap = [(d, d ^ 1) for d in range(subtrees)]
        their_who = lax.ppermute(grp_partner, "leaf", swap)
        their_blocks = lax.ppermute(grp_coupling, "leaf", swap)
        tall = vecs + 8
    else:
        hot = (grp_partner[0][:, None] == group_ids[None, :]).astype(bf16)
        by_partner = jnp.einsum("sh,sx->hx", hot, grp_coupling, preferred_element_type=f32)
        by_partner = by_partner.reshape(groups, rank, rank)
        self_hot = (group_ids == own_group).astype(f32)
        parts = (
            self_hot[:, None, None, None] * by_partner.transpose(1, 0, 2)[None]
            + self_hot[None, None, :, None] * by_partner.transpose(0, 2, 1)[:, :, None, :]
        )
        parts = parts.astype(bf16).reshape(groups, subtrees, 4 * rank).transpose(1, 0, 2)
        chunks = lax.all_to_all(parts, "leaf", 0, 0, tiled=True)
        chunk = chunks.astype(f32).sum(0)
        tall = vecs

    coeff, tops, backs, own_who, own_blocks = pl.pallas_call(
        up_kernel,
        out_shape=(
            made((leaves, vecs, rank), bf16),
            made((vecs, 2 * rank), f32),
            made((subtrees, vecs, rank), f32),
            made(grp_partner.shape, grp_partner.dtype),
            made(grp_coupling.shape, grp_coupling.dtype),
        ),
        in_specs=[pl.BlockSpec(memory_space=pl.ANY)] * 11,
        out_specs=(vmem,) * 5,
        scratch_shapes=[pltpu.SMEM(x.shape, x.dtype) for x in (leaf_sizes, dev_partner)]
        + [
            pltpu.VMEM(x.shape, x.dtype)
            for x in (
                vectors,
                morton_order,
                leaf_basis,
                leaf_transfer,
                mid_transfer,
                root_transfer,
                dev_coupling,
            )
        ]
        + [
            pltpu.SemaphoreType.DMA((11,)),
            pltpu.VMEM((vecs, points), f32),
            pltpu.VMEM((rank * pitch_of(leaves), rank), f32),
            pltpu.VMEM((rank * 8, rank), f32),
            pltpu.VMEM((rank * pitch_of(slots), rank), f32),
        ],
        cost_estimate=pl.CostEstimate(flops=2 << 30, bytes_accessed=1 << 20, transcendentals=0),
        name="up",
    )(
        leaf_sizes,
        dev_partner,
        vectors,
        morton_order,
        leaf_basis,
        leaf_transfer,
        mid_transfer,
        root_transfer,
        dev_coupling,
        grp_partner,
        grp_coupling,
    )
    if few:
        group_args = [keep(x) for x in (own_who, their_who, own_blocks, their_blocks)]
    else:
        group_args = [chunk]
    message = pl.pallas_call(
        functools.partial(pack_kernel, few=few),
        out_shape=jax.ShapeDtypeStruct((subtrees, tall, 4 * rank), bf16),
        in_specs=[vmem] * (2 + len(group_args)),
        out_specs=pl.BlockSpec(memory_space=pl.ANY),
        scratch_shapes=[
            pltpu.VMEM((subtrees, tall, 4 * rank), bf16),
            pltpu.VMEM((rank * 2 * grp_coupling.shape[0], rank), f32),
            pltpu.VMEM((groups, rank // 2, rank), f32),
            pltpu.SemaphoreType.DMA((groups,)),
        ],
        name="pack",
    )(keep(tops), keep(backs), *group_args)
    got = lax.all_to_all(message, "leaf", 0, 0, tiled=True)

    reach, near, dev_wide, root_map = pl.pallas_call(
        near_kernel,
        out_shape=(
            made((rank, points), bf16),
            made((vecs, points), f32),
            made((rank, subtrees * 4 * rank), bf16),
            made((rank, rank), bf16),
        ),
        in_specs=[smem] * 3 + [vmem] * 8,
        out_specs=(vmem,) * 4,
        scratch_shapes=[
            pltpu.VMEM((rank * pitch_of(leaves), rank), f32),
            pltpu.VMEM((rank * 8, rank), f32),
            pltpu.VMEM((rank * pitch_of(slots), rank), f32),
            pltpu.VMEM((rank * pitch_of(npairs), rank), f32),
            pltpu.VMEM((leaves, vecs, rank), f32),
            pltpu.VMEM((rank + vecs, points), f32),
            pltpu.VMEM((subtrees + 1, rank, 4 * rank), f32),
        ],
        cost_estimate=pl.CostEstimate(flops=4 << 30, bytes_accessed=4 << 20, transcendentals=0),
        name="near",
    )(
        leaf_sizes,
        leaf_pairs,
        dev_partner,
        keep(coeff),
        keep(morton_order),
        keep(leaf_basis),
        keep(leaf_transfer),
        keep(mid_transfer),
        keep(root_transfer),
        keep(dev_coupling),
        keep(leaf_coupling),
    )

    return pl.pallas_call(
        functools.partial(last_kernel, few=few),
        out_shape=jax.ShapeDtypeStruct((vecs, points), f32),
        in_specs=[vmem] * 5,
        out_specs=pl.BlockSpec(memory_space=pl.ANY),
        scratch_shapes=[
            pltpu.VMEM((8 if few else subtrees * tall, 4 * rank), f32),
            pltpu.VMEM((groups, vecs, rank), f32),
            pltpu.VMEM((vecs, points), f32),
            pltpu.SemaphoreType.DMA((4,)),
        ],
        name="last",
    )(
        keep(got),
        keep(dev_wide),
        keep(root_map),
        keep(reach),
        keep(near),
    )


def solution(mesh):
    in_specs = (
        P(None, "leaf"),
        P("leaf", None),
        P("leaf", None),
        P(None, "leaf"),
        P("leaf", None),
        P("leaf", None),
        P("leaf", None),
        P(None, "leaf"),
        P("leaf", None),
        P("leaf", None),
        P("leaf", None),
        P("leaf", None),
        P("leaf", None),
    )
    out_specs = P(None, "leaf")
    return jax.shard_map(body, mesh=mesh, in_specs=in_specs, out_specs=out_specs, check_vma=False)
```

```python
import functools

import jax
import jax.numpy as jnp
from jax import lax
from jax.experimental import pallas as pl
from jax.experimental.pallas import tpu as pltpu
from jax.sharding import PartitionSpec as P

LEAF = 256
SPLIT = 256

bf16 = jnp.bfloat16
f32 = jnp.float32


def dot(a, b, over):
    return lax.dot_general(a, b, (over, ((), ())), preferred_element_type=f32)


NN = ((1,), (0,))
NT = ((1,), (1,))
TN = ((0,), (0,))


def one_hot_low(morton, width):
    rows = lax.broadcasted_iota(jnp.int32, (SPLIT, width), 0).astype(bf16)
    low = (morton & (SPLIT - 1)).astype(f32).astype(bf16)
    return jnp.where(rows == low, jnp.ones((), bf16), jnp.zeros((), bf16))


def window(start, points, width):
    base = jnp.minimum(start - (start & 127), points - width)
    return pl.multiple_of(base, 128)


def inside_of(start, size, base, shape):
    place = lax.broadcasted_iota(jnp.int32, shape, 1) + (base - start)
    return place.astype(jnp.uint32) < size.astype(jnp.uint32)


def pitch_of(n):
    return n + 8 if n % 16 == 0 else n


def spread(scr, ref, row, pitch, rank):
    flat = ref[...].astype(f32)
    n = flat.shape[0]
    for i in range(rank):
        scr[i * pitch + row : i * pitch + row + n, :rank] = flat[:, rank * i : rank * (i + 1)]


def block_of(scr, n, pitch, rank):
    return scr[pl.ds(n, rank, stride=pitch), :][:, :rank].astype(bf16)


def beside(tiles):
    return jnp.concatenate(tiles, axis=1)


def up_kernel(
    sizes_hbm,
    partner_hbm,
    vec_hbm,
    morton_hbm,
    basis_hbm,
    leaf_hbm,
    mid_hbm,
    root_hbm,
    dev_hbm,
    who_hbm,
    group_hbm,
    coeff_ref,
    tops_ref,
    back_ref,
    who_ref,
    group_ref,
    sizes,
    partner,
    vec_ref,
    morton_ref,
    basis_ref,
    leaf_ref,
    mid_ref,
    root_ref,
    dev_ref,
    sems,
    sorted_ref,
    leaf_scr,
    scr,
    dev_scr,
):
    vecs, points = vec_ref.shape
    rank = basis_ref.shape[0]
    leaves = sizes.shape[1]
    middle = mid_ref.shape[0]
    slots = dev_ref.shape[0]
    highs = points // SPLIT
    width = min(points, LEAF + 128)
    basis_copy = pltpu.make_async_copy(basis_hbm, basis_ref, sems.at[1])
    copies = [
        pltpu.make_async_copy(src, dst, sems.at[0])
        for src, dst in (
            (vec_hbm, vec_ref),
            (morton_hbm, morton_ref),
            (sizes_hbm, sizes),
            (partner_hbm, partner),
            (who_hbm, who_ref),
            (mid_hbm, mid_ref),
            (root_hbm, root_ref),
            (leaf_hbm, leaf_ref),
            (dev_hbm, dev_ref),
            (group_hbm, group_ref),
        )
    ]
    for copy in copies:
        copy.start()
    basis_copy.start()
    for copy in copies:
        copy.wait()
    spread(leaf_scr, leaf_ref, 0, pitch_of(leaves), rank)
    spread(scr, mid_ref, 0, 8, rank)
    spread(scr, root_ref, middle, 8, rank)
    spread(dev_scr, dev_ref, 0, pitch_of(slots), rank)
    back_ref[...] = jnp.zeros_like(back_ref)
    stacked = jnp.concatenate(
        [vec_ref[:, h * SPLIT : (h + 1) * SPLIT].astype(bf16) for h in range(highs)], axis=0
    )
    step = 256
    for k in range(points // step):
        morton = morton_ref[:, k * step : (k + 1) * step]
        mixed = dot(stacked, one_hot_low(morton, step), NN)
        high = morton // SPLIT
        picked = mixed[:vecs]
        for h in range(1, highs):
            picked = jnp.where(high == h, mixed[h * vecs : (h + 1) * vecs], picked)
        sorted_ref[:, k * step : (k + 1) * step] = picked
    basis_copy.wait()
    start = jnp.int32(0)
    coeffs = []
    for l in range(leaves):
        size = sizes[0, l]
        base = window(start, points, width)
        inside = inside_of(start, size, base, (vecs, width))
        vec = jnp.where(inside, sorted_ref[:, pl.ds(base, width)], 0.0).astype(bf16)
        coeff = dot(vec, basis_ref[:, pl.ds(base, width)], NT)
        coeff_ref[l] = coeff.astype(bf16)
        coeffs.append(coeff)
        start = start + size
    mids = []
    for m in range(middle):
        kids = range(8 * m, 8 * m + 8)
        maps = [block_of(leaf_scr, l, pitch_of(leaves), rank) for l in kids]
        maps = jnp.concatenate(maps, axis=0)
        mids.append(dot(beside([coeffs[l] for l in kids]).astype(bf16), maps, NN))
    maps = jnp.concatenate([block_of(scr, m, 8, rank) for m in range(middle)], axis=0)
    root = dot(beside(mids).astype(bf16), maps, NN).astype(bf16)
    term = dot(root, block_of(scr, middle, 8, rank), NN)
    tops_ref[...] = beside([root.astype(f32), term])
    self_id = lax.axis_index("leaf")
    for c in range(slots):
        who = partner[0, c]
        back = dot(root, block_of(dev_scr, c, pitch_of(slots), rank), NN)
        back_ref[jnp.where(who >= 0, who, self_id)] = jnp.where(who >= 0, back, 0.0)


def pack_kernel(tops_ref, back_ref, *rest, few):
    group_refs, (msg_hbm, msg_ref, group_scr, half_scr, sems) = rest[:-5], rest[-5:]
    vecs = tops_ref.shape[0]
    rank = tops_ref.shape[1] // 2
    subtrees = msg_ref.shape[0]
    groups = subtrees // 8
    self_id = lax.axis_index("leaf")
    own = self_id // 8
    copies = []
    if few:
        held = group_refs[2].shape[0]
        pitch = 2 * held
        spread(group_scr, group_refs[2], 0, pitch, rank)
        spread(group_scr, group_refs[3], held, pitch, rank)
        half = rank // 2
        first = self_id % 2 * (half * pitch)
        sums = [jnp.zeros((half, rank), f32) for _ in range(groups)]
        for s in range(pitch):
            target = group_refs[s // held][:, s % held : s % held + 1]
            block = group_scr[pl.ds(first + s, half, stride=pitch), :][:, :rank]
            for h in range(groups):
                sums[h] = sums[h] + jnp.where(target == h, block, 0.0)
        for h in range(groups):
            half_scr[h] = sums[h]
        below = [half_scr[(own + 1 + q) % groups] for q in range(1, groups - 1)]
        below = beside([part for b in below for part in (b[:8], b[8:])]).astype(bf16)
    blank = jnp.zeros((vecs, rank), f32)
    for g in range(groups):
        if few:
            part = half_scr[jnp.where(own == g, (own + 1) % groups, g)]
        else:
            chunk = group_refs[0][g : g + 1, :]
            part = jnp.concatenate(
                [chunk[:, h * rank : (h + 1) * rank] for h in range(4)]
                + [jnp.zeros((vecs - 4, rank), f32)],
                axis=0,
            )
        tile = beside([tops_ref[...], blank, part]).astype(bf16)
        if few:
            tile = jnp.concatenate([tile, below], axis=0)
        for d in range(8 * g, 8 * g + 8):
            msg_ref[d] = tile
            msg_ref[d, :vecs, 2 * rank : 3 * rank] = back_ref[d].astype(bf16)
        some = pl.ds(8 * g, 8)
        copies.append(pltpu.make_async_copy(msg_ref.at[some], msg_hbm.at[some], sems.at[0]))
        copies[-1].start()
    for copy in copies:
        copy.wait()


def near_kernel(
    sizes,
    pairs,
    partner,
    coeff_ref,
    morton_ref,
    basis_ref,
    leaf_ref,
    mid_ref,
    root_ref,
    dev_ref,
    couple_ref,
    reach_ref,
    near_ref,
    dev_out,
    leaf_scr,
    scr,
    dev_scr,
    couple_scr,
    far_scr,
    sorted_ref,
    wide_scr,
):
    rank, points = basis_ref.shape
    leaves, vecs, _ = coeff_ref.shape
    middle = mid_ref.shape[0]
    slots = dev_ref.shape[0]
    npairs = couple_ref.shape[0]
    highs = points // SPLIT
    width = min(points, LEAF + 128)
    rows = rank + vecs
    spread(leaf_scr, leaf_ref, 0, pitch_of(leaves), rank)
    spread(scr, mid_ref, 0, 8, rank)
    spread(scr, root_ref, middle, 8, rank)
    spread(dev_scr, dev_ref, 0, pitch_of(slots), rank)
    spread(couple_scr, couple_ref, 0, pitch_of(npairs), rank)
    same = lax.broadcasted_iota(jnp.int32, (rank, 4 * rank), 1)
    same = same == lax.broadcasted_iota(jnp.int32, (rank, 4 * rank), 0) + 2 * rank
    same = jnp.where(same, 1.0, 0.0)
    subtrees = wide_scr.shape[0] - 1
    for b in range(subtrees):
        wide_scr[b] = same
    for c in range(slots):
        who = partner[0, c]
        block = dev_scr[pl.ds(c, rank, stride=pitch_of(slots)), :][:, :rank]
        wide_scr[jnp.where(who >= 0, who, subtrees), :, :rank] = block
    for b in range(subtrees):
        dev_out[:, 4 * rank * b : 4 * rank * (b + 1)] = wide_scr[b].astype(bf16)
    far_scr[...] = jnp.zeros_like(far_scr)
    for p in range(npairs):
        a = pairs[0, p]
        b = pairs[1, p]
        block = block_of(couple_scr, p, pitch_of(npairs), rank)
        to_a = dot(coeff_ref[b], block, NT)
        to_b = dot(coeff_ref[a], block, NN)
        far_scr[a] += to_a
        far_scr[b] += to_b
    start = jnp.int32(0)
    for l in range(leaves):
        size = sizes[0, l]
        base = window(start, points, width)
        inside = inside_of(start, size, base, (rows, width))
        reach = lax.dot_general(
            block_of(scr, l // 8, 8, rank),
            block_of(leaf_scr, l, pitch_of(leaves), rank),
            (((0,), (1,)), ((), ())),
            preferred_element_type=f32,
        )
        both = jnp.concatenate([reach, far_scr[l]], axis=0).astype(bf16)
        value = dot(both, basis_ref[:, pl.ds(base, width)], NN)
        old = sorted_ref[:, pl.ds(base, width)]
        sorted_ref[:, pl.ds(base, width)] = jnp.where(inside, value, old)
        start = start + size
    step = 256
    result = jnp.zeros((highs * rows, SPLIT), f32)
    for k in range(points // step):
        morton = morton_ref[:, k * step : (k + 1) * step]
        high = morton // SPLIT
        value = sorted_ref[:, k * step : (k + 1) * step]
        masked = jnp.concatenate([jnp.where(high == h, value, 0.0) for h in range(highs)], axis=0)
        result = result + dot(masked.astype(bf16), one_hot_low(morton, step), NT)
    for h in range(highs):
        reach = result[h * rows : h * rows + rank].astype(bf16)
        reach_ref[:rank, h * SPLIT : (h + 1) * SPLIT] = reach
        above = dot(block_of(scr, middle, 8, rank), reach, TN)
        reach_ref[rank:, h * SPLIT : (h + 1) * SPLIT] = above.astype(bf16)
        near_ref[:, h * SPLIT : (h + 1) * SPLIT] = result[h * rows + rank : (h + 1) * rows]


def last_kernel(
    got_ref,
    dev_ref,
    reach_ref,
    near_ref,
    out_hbm,
    got,
    group_scr,
    out_ref,
    sems,
    *,
    few,
):
    rank = dev_ref.shape[0]
    subtrees, tall, tile_lanes = got_ref.shape
    vecs = near_ref.shape[0]
    groups = subtrees // 8
    own = lax.axis_index("leaf") // 8
    total = dot(beside([got_ref[b][:vecs] for b in range(subtrees)]), dev_ref[...], NT)
    if not few:
        got[...] = got_ref[...].astype(f32).reshape(subtrees * tall, tile_lanes)
    far = jnp.zeros((vecs, rank), f32)
    for g in range(groups):
        level = got_ref[g * 8, :vecs].astype(f32)
        for d in range(1, 8):
            level = level + got_ref[g * 8 + d, :vecs].astype(f32)
        group = level[:, rank : 2 * rank]
        if few:
            group_scr[g] = group
        else:
            pitch = groups // 4
            block = got[pl.ds(g // 4 * vecs + g % 4, rank, stride=pitch * vecs), :]
            far = far + dot(group.astype(bf16), block[:, 3 * rank : 4 * rank].astype(bf16), NT)
    if few:

        def stack_of(g, q):
            halves = []
            for core in range(2):
                acc = 0.0
                for chip in range(4):
                    message = got_ref.at[g * 8 + 2 * chip + core]
                    if q == 0:
                        part = message[:vecs, 3 * rank :].astype(f32)
                    else:
                        part = message[vecs:, (q - 1) * 2 * rank : q * 2 * rank].astype(f32)
                    acc = acc + part
                halves.append(acc if q == 0 else jnp.concatenate([acc[:, :rank], acc[:, rank:]], axis=0))
            return jnp.concatenate(halves, axis=0).astype(bf16)

        for q in range(groups - 1):
            other = (own + 1 + q) % groups
            group = group_scr[other].astype(bf16)
            far = far + dot(group, stack_of(own, q), NT) + dot(group, stack_of(other, 0), NN)
    total = beside([total, far]).astype(bf16)
    points = near_ref.shape[1]
    pieces = 4
    copies = []
    for n in range(pieces):
        cols = pl.ds(n * (points // pieces), points // pieces)
        out_ref[:, cols] = near_ref[:, cols] + dot(total, reach_ref[:, cols], NN)
        copies.append(pltpu.make_async_copy(out_ref.at[:, cols], out_hbm.at[:, cols], sems.at[0]))
        copies[-1].start()
    for copy in copies:
        copy.wait()


smem = pl.BlockSpec(memory_space=pltpu.SMEM)
vmem = pl.BlockSpec(memory_space=pltpu.VMEM)


def on_chip(x):
    return pltpu.with_memory_space_constraint(x, pltpu.VMEM)


def body(
    vectors,
    morton_order,
    leaf_sizes,
    leaf_basis,
    leaf_transfer,
    mid_transfer,
    root_transfer,
    leaf_pairs,
    leaf_coupling,
    dev_partner,
    dev_coupling,
    grp_partner,
    grp_coupling,
):
    rank, points = leaf_basis.shape
    vecs = vectors.shape[0]
    leaves = leaf_sizes.shape[1]
    slots = dev_coupling.shape[0]
    npairs = leaf_coupling.shape[0]
    subtrees = lax.axis_size("leaf")
    groups = subtrees // 8
    few = groups == 4
    keep, made = (on_chip, pltpu.VMEM) if few else (lambda x: x, jax.ShapeDtypeStruct)
    self_id = lax.axis_index("leaf").astype(jnp.int32)
    own_group = self_id // 8
    group_ids = jnp.arange(groups, dtype=jnp.int32)
    if few:
        swap = [(d, d ^ 1) for d in range(subtrees)]
        their_who = lax.ppermute(grp_partner, "leaf", swap)
        their_blocks = lax.ppermute(grp_coupling, "leaf", swap)
        tall = vecs + 8
    else:
        hot = (grp_partner[0][:, None] == group_ids[None, :]).astype(bf16)
        by_partner = jnp.einsum("sh,sx->hx", hot, grp_coupling, preferred_element_type=f32)
        by_partner = by_partner.reshape(groups, rank, rank)
        self_hot = (group_ids == own_group).astype(f32)
        parts = (
            self_hot[:, None, None, None] * by_partner.transpose(1, 0, 2)[None]
            + self_hot[None, None, :, None] * by_partner.transpose(0, 2, 1)[:, :, None, :]
        )
        parts = parts.astype(bf16).reshape(groups, subtrees, 4 * rank).transpose(1, 0, 2)
        chunks = lax.all_to_all(parts, "leaf", 0, 0, tiled=True)
        chunk = chunks.astype(f32).sum(0)
        tall = vecs

    coeff, tops, backs, own_who, own_blocks = pl.pallas_call(
        up_kernel,
        out_shape=(
            made((leaves, vecs, rank), bf16),
            made((vecs, 2 * rank), f32),
            made((subtrees, vecs, rank), f32),
            made(grp_partner.shape, grp_partner.dtype),
            made(grp_coupling.shape, grp_coupling.dtype),
        ),
        in_specs=[pl.BlockSpec(memory_space=pl.ANY)] * 11,
        out_specs=(vmem,) * 5,
        scratch_shapes=[pltpu.SMEM(x.shape, x.dtype) for x in (leaf_sizes, dev_partner)]
        + [
            pltpu.VMEM(x.shape, x.dtype)
            for x in (
                vectors,
                morton_order,
                leaf_basis,
                leaf_transfer,
                mid_transfer,
                root_transfer,
                dev_coupling,
            )
        ]
        + [
            pltpu.SemaphoreType.DMA((2,)),
            pltpu.VMEM((vecs, points), f32),
            pltpu.VMEM((rank * pitch_of(leaves), rank), f32),
            pltpu.VMEM((rank * 8, rank), f32),
            pltpu.VMEM((rank * pitch_of(slots), rank), f32),
        ],
        cost_estimate=pl.CostEstimate(flops=2 << 30, bytes_accessed=1 << 20, transcendentals=0),
        name="up",
    )(
        leaf_sizes,
        dev_partner,
        vectors,
        morton_order,
        leaf_basis,
        leaf_transfer,
        mid_transfer,
        root_transfer,
        dev_coupling,
        grp_partner,
        grp_coupling,
    )
    if few:
        group_args = [keep(x) for x in (own_who, their_who, own_blocks, their_blocks)]
    else:
        group_args = [chunk]
    message = pl.pallas_call(
        functools.partial(pack_kernel, few=few),
        out_shape=jax.ShapeDtypeStruct((subtrees, tall, 4 * rank), bf16),
        in_specs=[vmem] * (2 + len(group_args)),
        out_specs=pl.BlockSpec(memory_space=pl.ANY),
        scratch_shapes=[
            pltpu.VMEM((subtrees, tall, 4 * rank), bf16),
            pltpu.VMEM((rank * 2 * grp_coupling.shape[0], rank), f32),
            pltpu.VMEM((groups, rank // 2, rank), f32),
            pltpu.SemaphoreType.DMA((1,)),
        ],
        name="pack",
    )(keep(tops), keep(backs), *group_args)
    got = lax.all_to_all(message, "leaf", 0, 0, tiled=True)

    reach, near, dev_wide = pl.pallas_call(
        near_kernel,
        out_shape=(
            made((2 * rank, points), bf16),
            made((vecs, points), f32),
            made((rank, subtrees * 4 * rank), bf16),
        ),
        in_specs=[smem] * 3 + [vmem] * 8,
        out_specs=(vmem,) * 3,
        scratch_shapes=[
            pltpu.VMEM((rank * pitch_of(leaves), rank), f32),
            pltpu.VMEM((rank * 8, rank), f32),
            pltpu.VMEM((rank * pitch_of(slots), rank), f32),
            pltpu.VMEM((rank * pitch_of(npairs), rank), f32),
            pltpu.VMEM((leaves, vecs, rank), f32),
            pltpu.VMEM((rank + vecs, points), f32),
            pltpu.VMEM((subtrees + 1, rank, 4 * rank), f32),
        ],
        cost_estimate=pl.CostEstimate(flops=4 << 30, bytes_accessed=4 << 20, transcendentals=0),
        name="near",
    )(
        leaf_sizes,
        leaf_pairs,
        dev_partner,
        keep(coeff),
        keep(morton_order),
        keep(leaf_basis),
        keep(leaf_transfer),
        keep(mid_transfer),
        keep(root_transfer),
        keep(dev_coupling),
        keep(leaf_coupling),
    )

    return pl.pallas_call(
        functools.partial(last_kernel, few=few),
        out_shape=jax.ShapeDtypeStruct((vecs, points), f32),
        in_specs=[vmem] * 4,
        out_specs=pl.BlockSpec(memory_space=pl.ANY),
        scratch_shapes=[
            pltpu.VMEM((8 if few else subtrees * tall, 4 * rank), f32),
            pltpu.VMEM((groups, vecs, rank), f32),
            pltpu.VMEM((vecs, points), f32),
            pltpu.SemaphoreType.DMA((1,)),
        ],
        name="last",
    )(
        keep(got),
        keep(dev_wide),
        keep(reach),
        keep(near),
    )


def solution(mesh):
    in_specs = (
        P(None, "leaf"),
        P("leaf", None),
        P("leaf", None),
        P(None, "leaf"),
        P("leaf", None),
        P("leaf", None),
        P("leaf", None),
        P(None, "leaf"),
        P("leaf", None),
        P("leaf", None),
        P("leaf", None),
        P("leaf", None),
        P("leaf", None),
    )
    out_specs = P(None, "leaf")
    return jax.shard_map(body, mesh=mesh, in_specs=in_specs, out_specs=out_specs, check_vma=False)
```
